32 devices in a mesh: grp: 4 (over x, core), dir: 8 (over z, y).
Axes of the slice: x: 2, y: 2, z: 4, core: 2. Of those that a mesh axis runs over, the one named last changes fastest.
Arguments:
- child_out: bfloat16 [512, 2, 8, 2048], P(('grp', 'dir')), may hold values from -6 to 6
- low_trans: bfloat16 [316, 2, 2048], replicated, may hold values from -0.59765625 to 0.59765625
- up_trans: bfloat16 [316, 2, 64, 128], P(None, None, 'dir'), may hold values from -0.41992188 to 0.41992188
- far_src: int32 [512, 96], P(('grp', 'dir')), may hold values from 0 to 15
- far_kind: int32 [512, 96], P(('grp', 'dir')), may hold values from 0 to 315
- far_len: int32 [512], P(('grp', 'dir')), may hold values from 1 to 96, as said below
- send_sel: int32 [4, 8, 8, 2], P('grp', 'dir'), may hold values from 0 to 15
- par_src: int32 [64, 96], P('grp'), may hold values from 0 to 31
- par_kind: int32 [64, 96], P('grp'), may hold values from 0 to 315
- par_len: int32 [64], P('grp'), may hold values from 1 to 96, as said below
- par_sel: int32 [4, 4, 8], replicated, may hold values from 0 to 15
Outputs:
- box_in: bfloat16 [512, 2, 8, 2048], P(('grp', 'dir'))
The draws below stay inside these ranges and needn't reach their ends.
Inputs may be any that keep to these rules, and one draw needn't show every extreme that they name: Entries at positions from far_len[b] on are padding. Entries at positions from par_len[q] on are padding.
All inputs are finite; a program needn't handle non-finite values.
Results may differ from the reference program's by a relative error of at most 0.0052.
Values may be sent and summed in bfloat16 or wider, within the bound.
No kernel may reach another device: no remote copies, remote signals or barrier semaphores. Data moves between devices by JAX's collectives and lax.ppermute only.
A program may use at most 128 MiB of HBM per device.

```python
import math
import jax
import jax.numpy as jnp
from jax import lax

B_DEV = 16
RHS = 8
TH1 = 32
PH1 = 64
TH2 = 64
PH2 = 128
KINDS = 316
CAP = 2
FAR = 96
FARP = 96
GROUPS = 4
PLACES = 8
DIRS1 = 2048
BOXES = 512
P_GRP = 16
PARENTS = 64
CAPP = 8
N_DIR = 8


def skewed_lengths(seed_key, count, block_size, most):
    first_key, second_key, third_key, fourth_key = jax.random.split(seed_key, 4)
    owners = count // block_size
    levels = jax.random.randint(first_key, (owners,), 0, 4)
    busiest = jax.random.randint(second_key, (), 0, owners)
    levels = jnp.where(jnp.arange(owners) == busiest, 0, levels).astype(jnp.int32)
    limits = jnp.right_shift(jnp.full((owners,), most, jnp.int32), levels)
    limits = jnp.repeat(limits, block_size)
    drawn = jax.random.randint(third_key, (count,), 0, 1 << 20)
    lengths = 1 + drawn % limits
    pinned = busiest * block_size + jax.random.randint(fourth_key, (), 0, block_size)
    return jnp.where(jnp.arange(count) == pinned, most, lengths).astype(jnp.int32)


def draw_far_len(key, part):
    return skewed_lengths(jax.random.fold_in(key, 17), BOXES, B_DEV, FAR)


def draw_par_len(key, part):
    return skewed_lengths(jax.random.fold_in(key, 29), PARENTS, P_GRP, FARP)


def plant(values, stream_key, smallest, high):
    place = [jax.random.randint(jax.random.fold_in(stream_key, axis), (), 0, length) for axis, length in enumerate(values.shape)]
    widest = values.shape.index(max(values.shape))
    next_to = place[:widest] + [(place[widest] + 1) % values.shape[widest]] + place[widest + 1:]
    return values.at[tuple(place)].set(smallest).at[tuple(next_to)].set(high)


def level_of(key, extent, cuts, least, high):
    def one(dim, blocks):
        steps = jax.random.uniform(jax.random.fold_in(jax.random.fold_in(key, 6), dim), (blocks,), jnp.float32, least / len(cuts), high / len(cuts))
        return jnp.repeat(jnp.exp(steps), extent[dim] // blocks).reshape((-1,) + (1,) * (len(extent) - dim - 1))

    factor_of = one(*cuts[0])
    for cut in cuts[1:]:
        factor_of = factor_of * one(*cut)
    return factor_of


def scatter_about(own_key, shape, scale, most, cuts=(), kind=jnp.bfloat16):
    array = jax.random.normal(own_key, shape, jnp.float32) * scale
    if len(cuts) > 0:
        array = level_of(own_key, shape, cuts, -0.22, 0.18) * array
    return jnp.clip(array, min=-most, max=most).astype(kind)


def setup_inputs(seed: int = 0) -> dict:
    streams_of = jax.random.split(jax.random.key(seed), 12)
    return {
        "child_out": scatter_about(streams_of[0], (BOXES, 2, RHS, DIRS1), 1.0, 6.0, ((0, 32),)),
        "low_trans": scatter_about(streams_of[1], (KINDS, 2, DIRS1), 0.1, 0.59765625),
        "up_trans": scatter_about(streams_of[2], (KINDS, 2, TH2, PH2), 0.07, 0.41992188, ((2, 8),)),
        "far_src": plant(jax.random.randint(streams_of[3], (BOXES, FAR), 0, PLACES * CAP), jax.random.fold_in(streams_of[3], 1), 0, (PLACES * CAP) - 1).astype(jnp.int32),
        "far_kind": plant(jax.random.randint(streams_of[4], (BOXES, FAR), 0, KINDS), jax.random.fold_in(streams_of[4], 1), 0, KINDS - 1).astype(jnp.int32),
        "far_len": draw_far_len(jax.random.fold_in(streams_of[11], 71), 0),
        "send_sel": plant(jax.random.randint(streams_of[6], (GROUPS, PLACES, PLACES, CAP), 0, B_DEV), jax.random.fold_in(streams_of[6], 1), 0, B_DEV - 1).astype(jnp.int32),
        "par_src": plant(jax.random.randint(streams_of[7], (PARENTS, FARP), 0, GROUPS * CAPP), jax.random.fold_in(streams_of[7], 1), 0, (GROUPS * CAPP) - 1).astype(jnp.int32),
        "par_kind": plant(jax.random.randint(streams_of[8], (PARENTS, FARP), 0, KINDS), jax.random.fold_in(streams_of[8], 1), 0, KINDS - 1).astype(jnp.int32),
        "par_len": draw_par_len(jax.random.fold_in(streams_of[11], 71), 0),
        "par_sel": plant(jax.random.randint(streams_of[10], (GROUPS, GROUPS, CAPP), 0, P_GRP), jax.random.fold_in(streams_of[10], 1), 0, P_GRP - 1).astype(jnp.int32),
    }


WAVE_NUMBER = 2.5


def interp_matrix(targets, sources):
    target_grid = jnp.arange(targets, dtype=jnp.float32) * (2.0 * math.pi / targets)
    source_grid = jnp.arange(sources, dtype=jnp.float32) * (2.0 * math.pi / sources)
    spacing = target_grid[:, None] - source_grid[None, :]
    harmonics = jnp.arange(1, sources // 2, dtype=jnp.float32)
    kernel = 1.0 + 2.0 * jnp.sum(jnp.cos(spacing[:, :, None] * harmonics), axis=2) + jnp.cos(spacing * (sources // 2))
    return kernel / sources


def phase_tables(rows, columns):
    polar_angle = (jnp.arange(rows, dtype=jnp.float32) + 0.5) * (math.pi / rows)
    azimuth = jnp.arange(columns, dtype=jnp.float32) * (2.0 * math.pi / columns)
    along_x = jnp.sin(polar_angle)[:, None] * jnp.cos(azimuth)[None, :]
    along_y = jnp.sin(polar_angle)[:, None] * jnp.sin(azimuth)[None, :]
    along_z = jnp.cos(polar_angle)[:, None] * jnp.ones((1, columns), jnp.float32)
    octant = jnp.arange(8, dtype=jnp.int32)
    sign_x = (2 * (octant % 2) - 1).astype(jnp.float32)[:, None, None]
    sign_y = (2 * ((octant // 2) % 2) - 1).astype(jnp.float32)[:, None, None]
    sign_z = (2 * ((octant // 4) % 2) - 1).astype(jnp.float32)[:, None, None]
    angles = WAVE_NUMBER * (sign_x * along_x + sign_y * along_y + sign_z * along_z)
    return jnp.cos(angles), jnp.sin(angles)


def aggregate(children):
    rows_up = interp_matrix(TH2, TH1)
    cols_up = interp_matrix(PH2, PH1)
    values = children.astype(jnp.float32)
    widened = jnp.einsum("cmrtp,qp->cmrtq", values, cols_up, precision=lax.Precision.HIGHEST)
    widened = jnp.einsum("st,cmrtq->cmrsq", rows_up, widened, precision=lax.Precision.HIGHEST)
    cosine, sine = phase_tables(TH2, PH2)
    real_part = jnp.sum(cosine[:, None] * widened[:, 0] - sine[:, None] * widened[:, 1], axis=0)
    imag_part = jnp.sum(cosine[:, None] * widened[:, 1] + sine[:, None] * widened[:, 0], axis=0)
    return jnp.stack([real_part, imag_part], 0).astype(jnp.bfloat16)


def disaggregate(parent):
    rows_up = interp_matrix(TH2, TH1)
    cols_up = interp_matrix(PH2, PH1)
    values = parent.astype(jnp.float32)
    cosine, sine = phase_tables(TH2, PH2)
    real_part = cosine[:, None] * values[0][None] + sine[:, None] * values[1][None]
    imag_part = cosine[:, None] * values[1][None] - sine[:, None] * values[0][None]
    shifted = jnp.stack([real_part, imag_part], 1)
    narrowed = jnp.einsum("st,cmrsq->cmrtq", rows_up, shifted, precision=lax.Precision.HIGHEST)
    narrowed = jnp.einsum("qp,cmrtq->cmrtp", cols_up, narrowed, precision=lax.Precision.HIGHEST)
    return narrowed * ((TH1 / TH2) * (PH1 / PH2))


def far_sum(sources, operator_table, source_index, kind_index, lengths, block_size):
    targets = source_index.shape[0]
    entries = source_index.shape[1]

    def accumulate(block_turn, totals):
        offset = block_turn * block_size
        picked = lax.dynamic_slice_in_dim(source_index, offset, block_size, 1)
        kind_block = lax.dynamic_slice_in_dim(kind_index, offset, block_size, 1)
        places = offset + jnp.arange(block_size, dtype=jnp.int32)
        live_mask = (places[None, :] < lengths[:, None]).astype(jnp.float32)
        operators = operator_table[kind_block].astype(jnp.float32)
        pieces = sources[picked].astype(jnp.float32)
        op_real = operators[:, :, 0]
        op_imag = operators[:, :, 1]
        live_mask = live_mask.reshape(live_mask.shape + (1,) * (op_real.ndim - 2))
        op_real = op_real * live_mask
        op_imag = op_imag * live_mask
        real_sum = jnp.sum(op_real[:, :, None] * pieces[:, :, 0] - op_imag[:, :, None] * pieces[:, :, 1], axis=1)
        imag_sum = jnp.sum(op_real[:, :, None] * pieces[:, :, 1] + op_imag[:, :, None] * pieces[:, :, 0], axis=1)
        return totals + jnp.stack([real_sum, imag_sum], 1)

    start_totals = jnp.zeros((targets, 2) + sources.shape[2:], jnp.float32)
    return lax.fori_loop(0, entries // block_size, accumulate, start_totals)


def reference(child_out, low_trans, up_trans, far_src, far_kind, far_len, send_sel, par_src, par_kind, par_len, par_sel):
    box_ids = jnp.arange(BOXES, dtype=jnp.int32)
    device_ids = box_ids // B_DEV
    groups = device_ids // N_DIR
    places = device_ids % N_DIR
    peer_ids = far_src // CAP
    slot_ids = far_src % CAP
    source_boxes = (groups[:, None] * N_DIR + peer_ids) * B_DEV + send_sel[groups[:, None], peer_ids, places[:, None], slot_ids]
    lower = far_sum(child_out, low_trans, source_boxes, far_kind, far_len, 1)
    parent_out = lax.map(aggregate, child_out.reshape(PARENTS, 8, 2, RHS, TH1, PH1))
    parent_ids = jnp.arange(PARENTS, dtype=jnp.int32)
    parent_groups = parent_ids // P_GRP
    anchor = par_src // CAPP
    anchor_slot = par_src % CAPP
    parent_sources = anchor * P_GRP + par_sel[anchor, parent_groups[:, None], anchor_slot]
    parent_in = far_sum(parent_out, up_trans, parent_sources, par_kind, par_len, 1).astype(jnp.bfloat16)
    spread = lax.map(disaggregate, parent_in)
    return (lower + spread.reshape(lower.shape)).astype(jnp.bfloat16)
```

```python
import functools
import math

import numpy as np

import jax
import jax.numpy as jnp
from jax import lax
from jax.experimental import pallas as pl
from jax.experimental.pallas import tpu as pltpu
from jax.sharding import PartitionSpec as P

TH1 = 32
PH1 = 64
TH2 = 64
PH2 = 128
WAVE_NUMBER = 2.5
LANES = 128


def interp_matrix(targets, sources):
    spacing = 2.0 * math.pi * (
        np.arange(targets)[:, None] / targets - np.arange(sources)[None, :] / sources
    )
    harmonics = np.arange(1, sources // 2)
    kernel = (
        1.0
        + 2.0 * np.sum(np.cos(spacing[:, :, None] * harmonics), axis=2)
        + np.cos(spacing * (sources // 2))
    )
    return kernel / sources


def phase_tables():
    polar = (np.arange(TH2) + 0.5) * (math.pi / TH2)
    azimuth = np.arange(PH2) * (2.0 * math.pi / PH2)
    along_x = np.sin(polar)[:, None] * np.cos(azimuth)[None, :]
    along_y = np.sin(polar)[:, None] * np.sin(azimuth)[None, :]
    along_z = np.cos(polar)[:, None] * np.ones((1, PH2))
    angles = []
    for c in range(4):
        sx, sy, sz = 2 * (c % 2) - 1, 2 * (c // 2 % 2) - 1, 2 * (c // 4 % 2) - 1
        angles.append(WAVE_NUMBER * (sx * along_x + sy * along_y + sz * along_z))
    angles = np.stack(angles)
    return np.cos(angles).astype(np.float32), np.sin(angles).astype(np.float32)


def vmem_call(kernel, out_shape, scratch, n_in, name):
    spec = pl.BlockSpec(memory_space=pltpu.VMEM)
    outs = jax.tree.map(lambda _: spec, out_shape)
    return pl.pallas_call(
        kernel,
        out_shape=out_shape,
        in_specs=[spec] * n_in,
        out_specs=outs,
        scratch_shapes=scratch,
        name=name,
    )


def aggregate_kernel(rhs, parents, x_ref, e1_ref, k1_ref, cos_ref, sin_ref, out_ref, w_ref):
    pairs = TH1 // 2

    def columns(j, carry):
        col = pl.multiple_of(j * LANES, LANES)
        wide = jnp.dot(
            x_ref[:, pl.ds(col, LANES)], e1_ref[...], preferred_element_type=jnp.float32
        )
        wide = wide.reshape(parents, 8, 2, rhs, 2, PH2)
        row = pl.multiple_of(j * 2 * rhs, 2 * rhs)
        for p in range(parents):
            for c in range(4):
                first, last = wide[p, c], wide[p, 7 - c]
                pieces = (
                    (0, 0, first[0] + last[0]),
                    (0, 1, first[1] + last[1]),
                    (1, 0, last[1] - first[1]),
                    (1, 1, first[0] - last[0]),
                )
                for which, half, value in pieces:
                    stacked = jnp.concatenate([value[:, 0], value[:, 1]], axis=0)
                    w_ref[p, c, which, pl.ds(row, 2 * rhs), half * PH2 : (half + 1) * PH2] = (
                        stacked.astype(jnp.bfloat16)
                    )
        return carry

    lax.fori_loop(0, pairs, columns, 0)
    dests = out_ref.shape[0]
    rows = TH2 // dests

    def one_parent(p, carry):
        total = None
        for c in range(4):
            for which, table in ((0, cos_ref), (1, sin_ref)):
                part = jnp.dot(k1_ref[...], w_ref[p, c, which], preferred_element_type=jnp.float32)
                factor = table[c]
                factor = jnp.concatenate([factor, factor], axis=1)[:, None, :]
                part = part.reshape(TH2, rhs, 2 * PH2) * factor
                total = part if total is None else total + part
        total = total.reshape(dests, rows * rhs, 2 * PH2).astype(jnp.bfloat16)
        for d in range(dests):
            out_ref[d, p] = total[d]
        return carry

    lax.fori_loop(0, parents, one_parent, 0)


def disaggregate_kernel(rhs, parents, z_ref, lower_ref, e2_ref, k2_ref, cos_ref, sin_ref, out_ref, l_ref):
    def one_parent(p, carry):
        dirs = z_ref.shape[0]
        z = jnp.concatenate([z_ref[d, p] for d in range(dirs)], axis=0).astype(jnp.float32)
        z = z.reshape(TH2, rhs, 2 * PH2)
        for c in range(4):
            narrow = []
            for table in (cos_ref, sin_ref):
                factor = table[c]
                factor = jnp.concatenate([factor, factor], axis=1)[:, None, :]
                turned = (z * factor).reshape(TH2 * rhs, 2 * PH2).astype(jnp.bfloat16)
                narrow.append(
                    jnp.dot(k2_ref[...], turned, preferred_element_type=jnp.float32)
                    .reshape(TH1, rhs, 2, PH2)
                )
            by_cos, by_sin = narrow
            for box, sign in ((c, 1.0), (7 - c, -1.0)):
                if sign > 0:
                    real = by_cos[:, :, 0] + by_sin[:, :, 1]
                    imag = by_cos[:, :, 1] - by_sin[:, :, 0]
                else:
                    real = by_cos[:, :, 0] - by_sin[:, :, 1]
                    imag = by_cos[:, :, 1] + by_sin[:, :, 0]
                both = jnp.concatenate([real, imag], axis=1).astype(jnp.bfloat16)
                row = pl.multiple_of((p * 8 + box) * 2 * rhs, 2 * rhs)
                for t in range(TH1):
                    half = t % 2
                    l_ref[t // 2, pl.ds(row, 2 * rhs), half * PH2 : (half + 1) * PH2] = both[t]
        return carry

    lax.fori_loop(0, parents, one_parent, 0)

    def columns(j, carry):
        col = pl.multiple_of(j * LANES, LANES)
        spread = jnp.dot(l_ref[j], e2_ref[...], preferred_element_type=jnp.float32)
        out_ref[:, pl.ds(col, LANES)] = (spread + lower_ref[:, pl.ds(col, LANES)]).astype(
            jnp.bfloat16
        )
        return carry

    lax.fori_loop(0, TH1 // 2, columns, 0)


def mix(w_ref, real_at, imag_at, target, first, count, column, imag_column, rhs):
    real = imag = None
    for i in range(count):
        row = first + i
        wr = w_ref[target, row : row + 1, pl.ds(column, LANES)]
        wi = w_ref[target, row : row + 1, pl.ds(imag_column, LANES)]
        wr = jnp.broadcast_to(wr, (rhs, LANES))
        wi = jnp.broadcast_to(wi, (rhs, LANES))
        re = wr * real_at[i] - wi * imag_at[i]
        im = wr * imag_at[i] + wi * real_at[i]
        real = re if real is None else real + re
        imag = im if imag is None else imag + im
    return real, imag


def lower_kernel(rhs, slots, w_ref, s_ref, out_ref):
    width = s_ref.shape[1]
    boxes = w_ref.shape[0]
    group = 16

    def columns(j, carry):
        col = pl.multiple_of(j * LANES, LANES)
        for base in range(0, slots, group):
            n = min(group, slots - base)
            block = s_ref[pl.ds(base * 2 * rhs, n * 2 * rhs), pl.ds(col, LANES)]
            block = block.astype(jnp.float32).reshape(n, 2, rhs, LANES)
            reals = [block[i, 0] for i in range(n)]
            imags = [block[i, 1] for i in range(n)]

            def one_box(b, inner):
                real, imag = mix(
                    w_ref, reals, imags, b, base, n, col, width + col, rhs
                )
                both = jnp.concatenate([real, imag], axis=0)
                row = pl.multiple_of(b * 2 * rhs, 2 * rhs)
                place = (pl.ds(row, 2 * rhs), pl.ds(col, LANES))
                if base:
                    both = both + out_ref[place]
                out_ref[place] = both
                return inner

            lax.fori_loop(0, boxes, one_box, 0)
        return carry

    lax.fori_loop(0, width // LANES, columns, 0)


def parent_kernel(rhs, slots, w_ref, s_ref, out_ref, acc_ref):
    rows = s_ref.shape[1] // rhs
    targets = w_ref.shape[0]
    group = 16

    def two_rows(j, carry):
        first = pl.multiple_of(j * 2 * rhs, 2 * rhs)
        for step in range(2):
            column = pl.multiple_of((j * 2 + step) * LANES, LANES)
            imag_column = column + rows * LANES
            for base in range(0, slots, group):
                n = min(group, slots - base)
                reals, imags = [], []
                for i in range(n):
                    block = s_ref[base + i, pl.ds(first, 2 * rhs), :].astype(jnp.float32)
                    block = block[step * rhs : (step + 1) * rhs]
                    reals.append(block[:, :LANES])
                    imags.append(block[:, LANES:])

                def one_target(q, inner):
                    real, imag = mix(
                        w_ref, reals, imags, q, base, n, column, imag_column, rhs
                    )
                    if base:
                        real = real + acc_ref[q, step, :, :LANES]
                        imag = imag + acc_ref[q, step, :, LANES:]
                    acc_ref[q, step, :, :LANES] = real
                    acc_ref[q, step, :, LANES:] = imag
                    return inner

                lax.fori_loop(0, targets, one_target, 0)

        def pack(q, inner):
            both = jnp.concatenate([acc_ref[q, 0], acc_ref[q, 1]], axis=0)
            out_ref[q, pl.ds(first, 2 * rhs), :] = both.astype(jnp.bfloat16)
            return inner

        lax.fori_loop(0, targets, pack, 0)
        return carry

    lax.fori_loop(0, rows // 2, two_rows, 0)


def pair_counts(source_index, kind_index, lengths, slot_count, kind_count):
    entries = source_index.shape[1]
    live = jnp.arange(entries, dtype=jnp.int32)[None, :] < lengths[:, None]
    slot_ids = jnp.arange(slot_count, dtype=jnp.int32)
    kind_ids = jnp.arange(kind_count, dtype=jnp.int32)
    hit_slot = ((source_index[:, :, None] == slot_ids) & live[:, :, None]).astype(jnp.bfloat16)
    hit_kind = (kind_index[:, :, None] == kind_ids).astype(jnp.bfloat16)
    counts = jnp.einsum("bjs,bjk->bsk", hit_slot, hit_kind, preferred_element_type=jnp.float32)
    return counts.astype(jnp.bfloat16).reshape(-1, kind_count)


def body(
    child_out,
    low_trans,
    up_trans,
    far_src,
    far_kind,
    far_len,
    send_sel,
    par_src,
    par_kind,
    par_len,
    par_sel,
):
    boxes_here, _, rhs, width = child_out.shape
    parents_here = boxes_here // 8
    dirs = lax.axis_size("dir")
    groups = lax.axis_size("grp")
    group_index = lax.axis_index("grp")
    kinds = low_trans.shape[0]
    rows_here = TH2 // dirs
    tall = 2 * PH2

    rows_up, cols_up = interp_matrix(TH2, TH1), interp_matrix(PH2, PH1)
    scale = TH1 / TH2 * (PH1 / PH2)
    bf = lambda a: jnp.asarray(a.astype(np.float32)).astype(jnp.bfloat16)
    e1 = bf(np.kron(np.eye(2), cols_up.T))
    k1 = bf(np.kron(rows_up, np.eye(rhs)))
    e2 = bf(np.kron(np.eye(2), cols_up) * scale)
    k2 = bf(np.kron(rows_up.T, np.eye(rhs)))
    cosine, sine = phase_tables()
    cosine, sine = jnp.asarray(cosine), jnp.asarray(sine)

    outgoing = child_out[send_sel[0, 0]]
    arrived = lax.all_to_all(outgoing, "dir", split_axis=0, concat_axis=0, tiled=True)
    low_slots = dirs * send_sel.shape[3]

    flat = child_out.reshape(boxes_here * 2 * rhs, width)
    parent_out = vmem_call(
        functools.partial(aggregate_kernel, rhs, parents_here),
        jax.ShapeDtypeStruct((dirs, parents_here, rows_here * rhs, tall), jnp.bfloat16),
        [pltpu.VMEM((parents_here, 4, 2, TH1 * rhs, tall), jnp.bfloat16)],
        5,
        "aggregate",
    )(flat, e1, k1, cosine, sine)
    sliced = lax.all_to_all(parent_out, "dir", split_axis=0, concat_axis=0, tiled=True)
    sliced = sliced.reshape((dirs * parents_here,) + sliced.shape[2:])
    offered = sliced[par_sel[group_index]]
    candidates = lax.all_to_all(offered, "grp", split_axis=0, concat_axis=0, tiled=True)
    up_slots = groups * par_sel.shape[2]
    candidates = candidates.reshape((up_slots,) + candidates.shape[2:])

    up_counts = pair_counts(par_src, par_kind, par_len, up_slots, kinds)
    up_weights = jnp.dot(
        up_counts, up_trans.reshape(kinds, -1), preferred_element_type=jnp.float32
    )
    targets = par_src.shape[0]
    parent_in = vmem_call(
        functools.partial(parent_kernel, rhs, up_slots),
        jax.ShapeDtypeStruct((targets, rows_here * rhs, tall), jnp.bfloat16),
        [pltpu.VMEM((targets, 2, rhs, tall), jnp.float32)],
        2,
        "parent_far",
    )(up_weights.reshape(targets, up_slots, -1), candidates)
    parent_in = parent_in.reshape(dirs, parents_here, rows_here * rhs, tall)
    returned = lax.all_to_all(parent_in, "dir", split_axis=0, concat_axis=0, tiled=True)

    low_counts = pair_counts(far_src, far_kind, far_len, low_slots, kinds)
    low_weights = jnp.dot(
        low_counts, low_trans.reshape(kinds, -1), preferred_element_type=jnp.float32
    )
    lower = vmem_call(
        functools.partial(lower_kernel, rhs, low_slots),
        jax.ShapeDtypeStruct((boxes_here * 2 * rhs, width), jnp.float32),
        [],
        2,
        "lower_far",
    )(low_weights.reshape(boxes_here, low_slots, -1), arrived.reshape(low_slots * 2 * rhs, width))

    out = vmem_call(
        functools.partial(disaggregate_kernel, rhs, parents_here),
        jax.ShapeDtypeStruct((boxes_here * 2 * rhs, width), jnp.bfloat16),
        [pltpu.VMEM((TH1 // 2, boxes_here * 2 * rhs, 2 * PH2), jnp.bfloat16)],
        6,
        "disaggregate",
    )(returned, lower, e2, k2, cosine, sine)
    return out.reshape(child_out.shape)


def solution(mesh):
    in_specs = (
        P(("grp", "dir"), None, None, None),
        P(),
        P(None, None, "dir", None),
        P(("grp", "dir"), None),
        P(("grp", "dir"), None),
        P(("grp", "dir")),
        P("grp", "dir", None, None),
        P("grp", None),
        P("grp", None),
        P("grp"),
        P(),
    )
    out_specs = P(("grp", "dir"), None, None, None)
    return jax.shard_map(body, mesh=mesh, in_specs=in_specs, out_specs=out_specs, check_vma=False)
```

```python
import functools
import math

import numpy as np

import jax
import jax.numpy as jnp
from jax import lax
from jax.experimental import pallas as pl
from jax.experimental.pallas import tpu as pltpu
from jax.sharding import PartitionSpec as P


TH1 = 32
PH1 = 64
TH2 = 64
PH2 = 128
WAVE_NUMBER = 2.5
LANES = 128
VMEM_LIMIT = 20 << 20


def interp_matrix(targets, sources):
    spacing = 2.0 * math.pi * (
        np.arange(targets)[:, None] / targets - np.arange(sources)[None, :] / sources
    )
    harmonics = np.arange(1, sources // 2)
    kernel = (
        1.0
        + 2.0 * np.sum(np.cos(spacing[:, :, None] * harmonics), axis=2)
        + np.cos(spacing * (sources // 2))
    )
    return kernel / sources


def phase_tables():
    polar = (np.arange(TH2) + 0.5) * (math.pi / TH2)
    azimuth = np.arange(PH2) * (2.0 * math.pi / PH2)
    along_x = np.sin(polar)[:, None] * np.cos(azimuth)[None, :]
    along_y = np.sin(polar)[:, None] * np.sin(azimuth)[None, :]
    along_z = np.cos(polar)[:, None] * np.ones((1, PH2))
    angles = []
    for c in range(4):
        sx, sy, sz = 2 * (c % 2) - 1, 2 * (c // 2 % 2) - 1, 2 * (c // 4 % 2) - 1
        angles.append(WAVE_NUMBER * (sx * along_x + sy * along_y + sz * along_z))
    angles = np.stack(angles)
    return np.cos(angles).astype(np.float32), np.sin(angles).astype(np.float32)


def vmem_call(kernel, out_shape, scratch, n_in, n_smem=0):
    spec = pl.BlockSpec(memory_space=pltpu.VMEM)
    outs = jax.tree.map(lambda _: spec, out_shape)
    return pl.pallas_call(
        kernel,
        out_shape=out_shape,
        in_specs=[pl.BlockSpec(memory_space=pltpu.SMEM)] * n_smem + [spec] * n_in,
        out_specs=outs,
        scratch_shapes=scratch,
        compiler_params=pltpu.CompilerParams(vmem_limit_bytes=VMEM_LIMIT),
    )


def select_kernel(send_ref, x_ref, *outs):
    place = lax.axis_index("dir")
    for k, out_ref in enumerate(outs):
        for i in range(out_ref.shape[0]):
            out_ref[i] = x_ref[send_ref[place ^ k, i]]


def weights_kernel(slots, axis, each, length_ref, source_ref, kind_ref, table_ref, out_ref, count_ref):
    targets, entries = source_ref.shape
    kinds = table_ref.shape[0]
    order = lax.broadcasted_iota(jnp.int32, (slots, entries), 0)
    slot_ids = ((order // each) ^ lax.axis_index(axis)) * each + order % each
    kind_ids = lax.broadcasted_iota(jnp.int32, (kinds, entries), 0)
    places = lax.broadcasted_iota(jnp.int32, (slots, entries), 1)
    for b in range(targets):
        source = jnp.broadcast_to(source_ref[b : b + 1, :], (slots, entries))
        kind = jnp.broadcast_to(kind_ref[b : b + 1, :], (kinds, entries))
        hit = (source == slot_ids) & (places < length_ref[b])
        hit_slot = jnp.where(hit, 1.0, 0.0).astype(jnp.bfloat16)
        hit_kind = jnp.where(kind == kind_ids, 1.0, 0.0).astype(jnp.bfloat16)
        counts = lax.dot_general(
            hit_slot, hit_kind, (((1,), (1,)), ((), ())), preferred_element_type=jnp.float32
        )
        count_ref[b * slots : (b + 1) * slots, :] = counts.astype(jnp.bfloat16)
    tile = 2 * LANES

    def columns(j, carry):
        place = rows_of(j, tile)
        value = jnp.dot(count_ref[...], table_ref[:, place], preferred_element_type=jnp.float32)
        out_ref[:, :, place] = value.reshape(targets, slots, tile)
        return carry

    lax.fori_loop(0, table_ref.shape[1] // tile, columns, 0)


def rows_of(index, size):
    return pl.ds(pl.multiple_of(index * size, size), size)


def aggregate_kernel(rhs, parents, dirs, x_ref, e1_ref, k1_ref, cos_ref, sin_ref, *refs):
    out_ref, w_ref, acc_ref = refs

    def columns(j, carry):
        wide = jnp.dot(
            x_ref[:, rows_of(j, LANES)], e1_ref[...], preferred_element_type=jnp.float32
        )
        place = rows_of(j, 2 * rhs)
        for p in range(parents):
            for c in range(4):
                first, last = (p * 8 + c) * 2 * rhs, (p * 8 + 7 - c) * 2 * rhs
                pick = lambda row, part: wide[row + part * rhs : row + (part + 1) * rhs]
                pieces = (
                    (0, 0, pick(first, 0) + pick(last, 0)),
                    (0, 1, pick(first, 1) + pick(last, 1)),
                    (1, 0, pick(last, 1) - pick(first, 1)),
                    (1, 1, pick(first, 0) - pick(last, 0)),
                )
                for which, half, value in pieces:
                    stacked = jnp.concatenate([value[:, :PH2], value[:, PH2:]], axis=0)
                    w_ref[p, c, which, place, half * PH2 : (half + 1) * PH2] = stacked.astype(
                        jnp.bfloat16
                    )
        return carry

    lax.fori_loop(0, TH1 // 2, columns, 0)

    def one_parent(p, carry):
        for c in range(4):
            parts = [
                jnp.dot(k1_ref[...], w_ref[p, c, which], preferred_element_type=jnp.float32)
                for which in range(2)
            ]
            for s in range(TH2):
                rows = slice(s * rhs, (s + 1) * rhs)
                fc = jnp.broadcast_to(cos_ref[c, s : s + 1, :], (rhs, PH2))
                fs = jnp.broadcast_to(sin_ref[c, s : s + 1, :], (rhs, PH2))
                for half in range(2):
                    lanes = slice(half * PH2, (half + 1) * PH2)
                    value = parts[0][rows, lanes] * fc + parts[1][rows, lanes] * fs
                    if c:
                        value = value + acc_ref[rows, lanes]
                    acc_ref[rows, lanes] = value
        size = TH2 // dirs * rhs
        for k in range(dirs):
            out_ref[k, p] = acc_ref[k * size : (k + 1) * size, :].astype(jnp.bfloat16)
        return carry

    lax.fori_loop(0, parents, one_parent, 0)


def offer_kernel(pick_ref, in_ref, *outs):
    group = lax.axis_index("grp")
    for k, out_ref in enumerate(outs):
        for i in range(out_ref.shape[0]):
            out_ref[i] = in_ref[pick_ref[group, group ^ k, i]]


def disaggregate_kernel(
    rhs, in_ref, lower_ref, e2_ref, k2_ref, cos_ref, sin_ref, out_ref, z_ref, turn_ref, l_ref
):
    dirs, parents, size, _ = in_ref.shape
    for k in range(dirs):
        for p in range(parents):
            z_ref[p, k * size : (k + 1) * size, :] = in_ref[k, p].astype(jnp.float32)

    def one_parent(p, carry):
        for c in range(4):
            for s in range(0, TH2, 2):
                rows = slice(s * rhs, (s + 2) * rhs)
                for which, table in ((0, cos_ref), (1, sin_ref)):
                    factor = [
                        jnp.broadcast_to(table[c, s + i : s + i + 1, :], (rhs, PH2))
                        for i in range(2)
                    ]
                    factor = jnp.concatenate(factor, axis=0)
                    for half in range(2):
                        lanes = slice(half * PH2, (half + 1) * PH2)
                        turn_ref[which, rows, lanes] = (z_ref[p, rows, lanes] * factor).astype(
                            jnp.bfloat16
                        )
            by_cos, by_sin = [
                jnp.dot(k2_ref[...], turn_ref[which], preferred_element_type=jnp.float32)
                for which in range(2)
            ]
            cr, ci = by_cos[:, :PH2], by_cos[:, PH2:]
            sr, si = by_sin[:, :PH2], by_sin[:, PH2:]
            for box, real, imag in ((c, cr + si, ci - sr), (7 - c, cr - si, ci + sr)):
                place = rows_of(p * 8 + box, 2 * rhs)
                for t in range(TH1):
                    rows = slice(t * rhs, (t + 1) * rhs)
                    both = jnp.concatenate([real[rows], imag[rows]], axis=0)
                    half = t % 2
                    l_ref[t // 2, place, half * PH2 : (half + 1) * PH2] = both.astype(jnp.bfloat16)
        return carry

    lax.fori_loop(0, parents, one_parent, 0)

    def columns(j, carry):
        place = rows_of(j, LANES)
        spread = jnp.dot(l_ref[j], e2_ref[...], preferred_element_type=jnp.float32)
        out_ref[:, place] = (spread + lower_ref[:, place]).astype(jnp.bfloat16)
        return carry

    lax.fori_loop(0, TH1 // 2, columns, 0)


def weight_sums(w_ref, extra_ref, column, imag_column, slots, group):
    targets = w_ref.shape[0]

    def one(b, carry):
        for first in range(slots.start, slots.stop, group):
            rows = slice(first, first + group)
            real = w_ref[b, rows, pl.ds(column, LANES)]
            imag = w_ref[b, rows, pl.ds(imag_column, LANES)]
            extra_ref[b, 0, rows, :] = real + imag
            extra_ref[b, 1, rows, :] = imag - real
        return carry

    lax.fori_loop(0, targets, one, 0, unroll=4)


def mix(w_ref, extra_ref, target, first, column, sources):
    sums = [None] * 3
    for i, (real, imag, both) in enumerate(sources):
        rows = slice(first + i, first + i + 1)
        factors = (
            w_ref[target, rows, pl.ds(column, LANES)],
            extra_ref[target, 0, rows, :],
            extra_ref[target, 1, rows, :],
        )
        for n, (factor, value) in enumerate(zip(factors, (both, imag, real))):
            term = jnp.broadcast_to(factor, value.shape) * value
            sums[n] = term if sums[n] is None else sums[n] + term
    return sums[0] - sums[1], sums[0] + sums[2]


def lower_kernel(rhs, dirs, w_ref, *refs):
    ins, out_ref, extra_ref = refs[:dirs], refs[dirs], refs[dirs + 1]
    width = out_ref.shape[1]
    boxes, slots = w_ref.shape[:2]
    each = slots // dirs
    group = 8

    def columns(j, carry):
        place = rows_of(j, LANES)
        column = pl.multiple_of(j * LANES, LANES)
        weight_sums(w_ref, extra_ref, column, column + width, range(slots), group)
        for base in range(0, slots, group):
            sources = []
            for slot in range(base, base + group):
                row = slot % each * 2 * rhs
                block = ins[slot // each][row : row + 2 * rhs, place].astype(jnp.float32)
                real, imag = block[:rhs], block[rhs:]
                sources.append((real, imag, real + imag))

            def one_box(b, inner):
                real, imag = mix(w_ref, extra_ref, b, base, column, sources)
                both = jnp.concatenate([real, imag], axis=0)
                rows = rows_of(b, 2 * rhs)
                if base:
                    both = both + out_ref[rows, place]
                out_ref[rows, place] = both
                return inner

            lax.fori_loop(0, boxes, one_box, 0, unroll=4)
        return carry

    lax.fori_loop(0, width // LANES, columns, 0)


def parent_kernel(rhs, first_slot, last, n_in, w_ref, *refs):
    ins, refs = refs[:n_in], refs[n_in:]
    before = None
    if last:
        before, refs = refs[0], refs[1:]
    outs, (extra_ref, acc_ref) = refs[:-2], refs[-2:]
    targets = w_ref.shape[0]
    group = ins[0].shape[0]
    rows = ins[0].shape[1] // rhs
    slots = range(first_slot, first_slot + n_in * group)

    def two_rows(j, carry):
        place = rows_of(j, 2 * rhs)
        for step in range(2):
            column = pl.multiple_of((j * 2 + step) * LANES, LANES)
            weight_sums(w_ref, extra_ref, column, column + rows * LANES, slots, group)
            for n in range(n_in):
                sources = []
                for i in range(group):
                    block = ins[n][i, place, :].astype(jnp.float32)
                    block = block[step * rhs : (step + 1) * rhs]
                    real, imag = block[:, :LANES], block[:, LANES:]
                    sources.append((real, imag, real + imag))

                def one_target(q, inner):
                    slot = first_slot + n * group
                    real, imag = mix(w_ref, extra_ref, q, slot, column, sources)
                    if n:
                        real = real + acc_ref[q, step, :, :LANES]
                        imag = imag + acc_ref[q, step, :, LANES:]
                    acc_ref[q, step, :, :LANES] = real
                    acc_ref[q, step, :, LANES:] = imag
                    return inner

                lax.fori_loop(0, targets, one_target, 0, unroll=4)

        each = targets // len(outs)
        for q in range(targets):
            both = jnp.concatenate([acc_ref[q, 0], acc_ref[q, 1]], axis=0)
            if last:
                both = both + before[q, place, :]
            out_ref = outs[q // each]
            out_ref[q % each, place, :] = both.astype(out_ref.dtype)
        return carry

    lax.fori_loop(0, rows // 2, two_rows, 0)


def pair_weights(source_index, kind_index, lengths, slots, axis, table):
    targets = source_index.shape[0]
    kinds, width = table.shape
    return vmem_call(
        functools.partial(weights_kernel, slots, axis, slots // lax.axis_size(axis)),
        jax.ShapeDtypeStruct((targets, slots, width), jnp.float32),
        [pltpu.VMEM((targets * slots, kinds), jnp.bfloat16)],
        3,
        1,
    )(lengths, source_index, kind_index, table)


def swap(value, axis, step):
    count = lax.axis_size(axis)
    return lax.ppermute(value, axis, [(i, i ^ step) for i in range(count)])


def body(
    child_out,
    low_trans,
    up_trans,
    far_src,
    far_kind,
    far_len,
    send_sel,
    par_src,
    par_kind,
    par_len,
    par_sel,
):
    boxes_here, _, rhs, width = child_out.shape
    parents = boxes_here // 8
    dirs, groups = lax.axis_size("dir"), lax.axis_size("grp")
    kinds = low_trans.shape[0]
    rows_here = TH2 // dirs
    tall = 2 * PH2
    slab = (rows_here * rhs, tall)

    rows_up, cols_up = interp_matrix(TH2, TH1), interp_matrix(PH2, PH1)
    scale = TH1 / TH2 * (PH1 / PH2)
    bf = lambda a: jnp.asarray(a.astype(np.float32)).astype(jnp.bfloat16)
    e1 = bf(np.kron(np.eye(2), cols_up.T))
    k1 = bf(np.kron(rows_up, np.eye(rhs)))
    e2 = bf(np.kron(np.eye(2), cols_up) * scale)
    k2 = bf(np.kron(rows_up.T, np.eye(rhs)))
    cosine, sine = phase_tables()
    cosine, sine = jnp.asarray(cosine), jnp.asarray(sine)

    cap = send_sel.shape[3]
    low_slots = dirs * cap
    leaving = vmem_call(
        select_kernel,
        [jax.ShapeDtypeStruct((cap,) + child_out.shape[1:], child_out.dtype)] * dirs,
        [],
        1,
        1,
    )(send_sel.reshape(dirs, cap), child_out)
    early = tuple(range(1, dirs // 2))
    arrived = {0: leaving[0]}
    for k in early:
        arrived[k] = swap(leaving[k], "dir", k)

    flat = child_out.reshape(boxes_here * 2 * rhs, width)
    parent_out = vmem_call(
        functools.partial(aggregate_kernel, rhs, parents, dirs),
        jax.ShapeDtypeStruct((dirs, parents) + slab, jnp.bfloat16),
        [
            pltpu.VMEM((parents, 4, 2, TH1 * rhs, tall), jnp.bfloat16),
            pltpu.VMEM((TH2 * rhs, tall), jnp.float32),
        ],
        5,
    )(flat, e1, k1, cosine, sine)
    sliced = lax.all_to_all(parent_out, "dir", split_axis=0, concat_axis=0, tiled=True)

    offers = par_sel.shape[2]
    up_slots = groups * offers
    up_weights = pair_weights(
        par_src, par_kind, par_len, up_slots, "grp", up_trans.reshape(kinds, -1)
    )
    targets = par_src.shape[0]
    low_weights = pair_weights(
        far_src, far_kind, far_len, low_slots, "dir", low_trans.reshape(kinds, -1)
    )
    sliced, up_weights = lax.optimization_barrier((sliced, up_weights))

    offered = vmem_call(
        offer_kernel, [jax.ShapeDtypeStruct((offers,) + slab, jnp.bfloat16)] * groups, [], 1, 1
    )(par_sel, sliced.reshape((dirs * parents,) + slab))
    late = [k for k in range(1, dirs) if k not in early]
    held = [leaving[k] for k in late]
    offered, held = lax.optimization_barrier((offered, held))
    candidates = [offered[0]]
    for k in range(1, groups):
        candidates.append(swap(offered[k], "grp", k))
    for k, block in zip(late, held):
        arrived[k] = swap(block, "dir", k)

    near = groups // 2
    partial_shape = jax.ShapeDtypeStruct((targets,) + slab, jnp.float32)
    scratch = [
        pltpu.VMEM((targets, 2, up_slots, LANES), jnp.float32),
        pltpu.VMEM((targets, 2, rhs, tall), jnp.float32),
    ]
    started = vmem_call(
        functools.partial(parent_kernel, rhs, 0, False, near), [partial_shape], scratch, 1 + near
    )(up_weights, *candidates[:near])
    parent_in = vmem_call(
        functools.partial(parent_kernel, rhs, near * offers, True, groups - near),
        [jax.ShapeDtypeStruct((targets,) + slab, jnp.bfloat16)],
        scratch,
        2 + groups - near,
    )(up_weights, *candidates[near:], *started)
    parent_in = parent_in[0].reshape((dirs, parents) + slab)
    returned = lax.all_to_all(parent_in, "dir", split_axis=0, concat_axis=0, tiled=True)

    shape = (cap * 2 * rhs, width)
    lower = vmem_call(
        functools.partial(lower_kernel, rhs, dirs),
        jax.ShapeDtypeStruct((boxes_here * 2 * rhs, width), jnp.float32),
        [pltpu.VMEM((boxes_here, 2, low_slots, LANES), jnp.float32)],
        1 + dirs,
    )(low_weights, *[arrived[k].reshape(shape) for k in range(dirs)])

    out = vmem_call(
        functools.partial(disaggregate_kernel, rhs),
        jax.ShapeDtypeStruct((boxes_here * 2 * rhs, width), jnp.bfloat16),
        [
            pltpu.VMEM((parents, TH2 * rhs, tall), jnp.float32),
            pltpu.VMEM((2, TH2 * rhs, tall), jnp.bfloat16),
            pltpu.VMEM((TH1 // 2, boxes_here * 2 * rhs, tall), jnp.bfloat16),
        ],
        6,
    )(returned, lower, e2, k2, cosine, sine)
    return out.reshape(child_out.shape)


def solution(mesh):
    in_specs = (
        P(("grp", "dir"), None, None, None),
        P(),
        P(None, None, "dir", None),
        P(("grp", "dir"), None),
        P(("grp", "dir"), None),
        P(("grp", "dir")),
        P("grp", "dir", None, None),
        P("grp", None),
        P("grp", None),
        P("grp"),
        P(),
    )
    out_specs = P(("grp", "dir"), None, None, None)

    return jax.shard_map(body, mesh=mesh, in_specs=in_specs, out_specs=out_specs, check_vma=False)
```
